32 devices in a mesh: scan: 2 (over x), row: 16 (over z, y, core).
Axes of the slice: x: 2, y: 2, z: 4, core: 2. Of those that a mesh axis runs over, the one named last changes fastest.
Arguments:
- object_field: float32 [2, 2, 4096, 768], P(None, None, ('scan', 'row')), parts along dimension 2, may hold values from -1 to 1
- row_offset: int32 [32], P(('scan', 'row')), parts along dimension 0, may hold values from 0 to 127
- col_offset: int32 [32], P(('scan', 'row')), parts along dimension 0, may hold values from 0 to 256
- amplitudes: float32 [32, 512, 512], P(('scan', 'row')), parts along dimension 0, may hold values from 0.2 to 2
- probe: float32 [4, 512, 512], P('scan'), parts along dimension 0, may hold values from -6 to 6
- phase: float32 [512, 512], replicated, may hold values from -3.140625 to 3.140625
Outputs:
- updated_object: float32 [2, 2, 4096, 768], P(None, None, ('scan', 'row')), parts along dimension 2
The draws below stay inside these ranges and needn't reach their ends.
There are 2 independent parts, one for each index of `scan`. The reference program is written for one: setup_inputs(seed, part) draws one part's arguments, and reference() takes and returns one part's arrays. A program takes and returns all parts, laid end to end along the dimension named above; an argument that names none is the same for every part. Nothing has to cross between parts.
All inputs are finite; a program needn't handle non-finite values.
Results may differ from the reference program's by a relative error of at most 0.014.
Values sent between devices are 32-bit elements; how exact they have to be, the bound alone decides.
A program may use at most 64 MiB of HBM per device.

```python
import math
import jax
import jax.numpy as jnp
from jax import lax

P_SIZE = 512
STRIP = 128
COLS = 768
NY = 2048
N_ROW = 16


def plant(array, stream_key, low, high):
    longest = array.shape.index(max(array.shape))
    spots = []
    for shift in (0, 1):
        where = [jax.random.randint(jax.random.fold_in(stream_key, axis), (), 0, length) for axis, length in enumerate(array.shape)]
        where[longest] = (where[longest] + shift) % array.shape[longest]
        spots.append(tuple(where))
    return array.at[spots[0]].set(low).at[spots[1]].set(high)


def steps_of(rng, shape, pieces, smallest, top_value):
    gain, own = 1.0, jax.random.fold_in(rng, 6)
    for axis_at, shards_of in pieces:
        heights = jnp.exp(jax.random.uniform(jax.random.fold_in(own, axis_at), (shards_of,), jnp.float32, smallest / len(pieces), top_value / len(pieces)))
        gain = gain * jnp.repeat(heights, shape[axis_at] // shards_of).reshape([-1 if axis == axis_at else 1 for axis in range(len(shape))])
    return gain


def scatter_about(rng, shape, scale, limit, kind=jnp.bfloat16):
    result = scale * jax.random.normal(rng, shape, jnp.float32)
    return jnp.clip(result, min=-limit, max=limit).astype(kind)


def setup_inputs(seed: int = 0, part: int = 0) -> dict:
    arg_keys = jax.random.split(jax.random.key(seed), 7)
    part_splits = jax.random.split(jax.random.fold_in(arg_keys[6], part), 7)
    object_field = jnp.clip(jax.random.uniform(part_splits[0], (2, 2, NY, COLS), jnp.float32, -1.0, 1.0) * steps_of(part_splits[0], (2, 2, NY, COLS), ((2, 16),), -0.4, 0.0), -1.0, 1.0)
    row_offset = plant(jax.random.randint(part_splits[1], (N_ROW,), 0, STRIP), jax.random.fold_in(part_splits[1], 1), 0, STRIP - 1).astype(jnp.int32)
    col_offset = plant(jax.random.randint(part_splits[2], (N_ROW,), 0, COLS - P_SIZE + 1), jax.random.fold_in(part_splits[2], 1), 0, COLS - P_SIZE).astype(jnp.int32)
    amplitudes = jnp.clip(0.2 + 1.8 * jax.random.uniform(part_splits[3], (N_ROW, P_SIZE, P_SIZE), jnp.float32) ** steps_of(part_splits[3], (N_ROW, P_SIZE, P_SIZE), ((0, 16),), -0.2, 0.2), 0.2, 2.0)
    probe = scatter_about(part_splits[4], (2, P_SIZE, P_SIZE), 1.0, 6.0, jnp.float32)
    phase = jnp.clip(jax.random.uniform(arg_keys[5], (P_SIZE, P_SIZE), jnp.float32, -3.140625, 3.140625), -3.140625, 3.140625)
    return {"object_field": object_field, "row_offset": row_offset, "col_offset": col_offset, "amplitudes": amplitudes, "probe": probe, "phase": phase}


def dft_mats(length, flip):
    index = jnp.arange(length, dtype=jnp.int32)
    angles = (index[:, None] * index[None, :] % length).astype(jnp.float32) * (-2.0 * math.pi / length)
    factor = 1.0 / math.sqrt(length)
    cos_table = (jnp.cos(angles) * factor).astype(jnp.bfloat16)
    sin_table = (jnp.sin(angles) * factor).astype(jnp.bfloat16)
    if flip:
        sin_table = -sin_table
    left_real = jnp.concatenate([cos_table, -sin_table], axis=1)
    left_imag = jnp.concatenate([sin_table, cos_table], axis=1)
    right_real = jnp.concatenate([cos_table, -sin_table], axis=0)
    right_imag = jnp.concatenate([sin_table, cos_table], axis=0)
    return (left_real, left_imag, right_real, right_imag)

def transform(real_part, imag_part, mats):
    left_real, left_imag, right_real, right_imag = mats
    stacked = jnp.concatenate([real_part.astype(jnp.bfloat16), imag_part.astype(jnp.bfloat16)], axis=0)
    half_real = jnp.dot(left_real, stacked, preferred_element_type=jnp.float32).astype(jnp.bfloat16)
    half_imag = jnp.dot(left_imag, stacked, preferred_element_type=jnp.float32).astype(jnp.bfloat16)
    joined = jnp.concatenate([half_real, half_imag], axis=1)
    return (jnp.dot(joined, right_real, preferred_element_type=jnp.float32), jnp.dot(joined, right_imag, preferred_element_type=jnp.float32))

def cmul(a_real, a_imag, b_real, b_imag):
    return (a_real * b_real - a_imag * b_imag, a_real * b_imag + a_imag * b_real)

def cmul_conj(a_real, a_imag, b_real, b_imag):
    return (a_real * b_real + a_imag * b_imag, a_real * b_imag - a_imag * b_real)

def window_gradient(window, probe, amplitude, phase, forward, inverse):
    prop_real = jnp.cos(phase)
    prop_imag = jnp.sin(phase)
    probe_real, probe_imag = (probe[0], probe[1])
    first_real, first_imag = (window[0, 0], window[0, 1])
    second_real, second_imag = (window[1, 0], window[1, 1])
    exit_real, exit_imag = cmul(probe_real, probe_imag, first_real, first_imag)
    freq_real, freq_imag = transform(exit_real, exit_imag, forward)
    moved_real, moved_imag = cmul(freq_real, freq_imag, prop_real, prop_imag)
    inner_real, inner_imag = transform(moved_real, moved_imag, inverse)
    wave_real, wave_imag = cmul(inner_real, inner_imag, second_real, second_imag)
    far_real, far_imag = transform(wave_real, wave_imag, forward)
    modulus = jnp.sqrt(far_real * far_real + far_imag * far_imag)
    ratio = amplitude / jnp.maximum(modulus, 0.1)
    resid_real = far_real * (1.0 - ratio)
    resid_imag = far_imag * (1.0 - ratio)
    back_real, back_imag = transform(resid_real, resid_imag, inverse)
    grad2_real, grad2_imag = cmul_conj(inner_real, inner_imag, back_real, back_imag)
    mid_real, mid_imag = cmul_conj(second_real, second_imag, back_real, back_imag)
    spec_real, spec_imag = transform(mid_real, mid_imag, forward)
    unprop_real, unprop_imag = cmul_conj(prop_real, prop_imag, spec_real, spec_imag)
    entry_real, entry_imag = transform(unprop_real, unprop_imag, inverse)
    grad1_real, grad1_imag = cmul_conj(probe_real, probe_imag, entry_real, entry_imag)
    return jnp.stack([jnp.stack([grad1_real, grad1_imag]), jnp.stack([grad2_real, grad2_imag])])

def reference(object_field, row_offset, col_offset, amplitudes, probe, phase):
    forward = dft_mats(P_SIZE, False)
    inverse = dft_mats(P_SIZE, True)
    span = jnp.arange(P_SIZE, dtype=jnp.int32)

    def window_rows(device, offset):
        return (device * STRIP + offset + STRIP // 2 - 2 * STRIP + span + NY) % NY

    def one_device(items):
        device, offset, column, amplitude = items
        rows = window_rows(device, offset)
        taken = jnp.take(object_field, rows, axis=2)
        window = lax.dynamic_slice_in_dim(taken, column, P_SIZE, axis=3)
        return window_gradient(window, probe, amplitude, phase, forward, inverse)
    devices = jnp.arange(N_ROW, dtype=jnp.int32)
    grads = lax.map(one_device, (devices, row_offset, col_offset, amplitudes))

    def place(device, canvas):
        rows = window_rows(device, row_offset[device])
        columns = col_offset[device] + span
        return canvas.at[:, :, rows[:, None], columns[None, :]].add(grads[device])
    canvas = lax.fori_loop(0, N_ROW, place, jnp.zeros_like(object_field))
    return object_field - 0.5 * canvas
```

```python
import functools
import math

import jax
import jax.numpy as jnp
from jax import lax
from jax.experimental import pallas as pl
from jax.experimental.pallas import tpu as pltpu
from jax.sharding import PartitionSpec as P

MESH = pl.DeviceIdType.MESH

M2, M1, OWN, P1, P2, P3 = range(6)
EDGES = {
    0: (
        (OWN, 0, "y", M2), (OWN, 1, -3, P3), (OWN, 0, "c", M1),
        (P2, 2, 4, M2), (P2, 0, "c", P1), (M1, 2, "c", M2),
    ),
    1: (
        (OWN, 0, "y", M2), (OWN, 0, "c", P1),
        (P2, 0, 3, M1), (P2, 1, "c", P3),
    ),
    2: (
        (OWN, 0, "y", P2), (OWN, 1, -3, P3), (OWN, 0, "c", M1),
        (M2, 0, -4, P2), (P2, 0, "c", P1),
    ),
    3: (
        (OWN, 0, "y", P2), (OWN, 0, "c", P1),
        (M2, 0, -4, P2), (M2, 0, "c", M1), (P2, 1, "c", P3),
    ),
}
BACK = {"y": "y", "c": "c", 3: -3, -3: 3, 4: -4, -4: 4}
MAX_EDGES = max(len(edges) for edges in EDGES.values())


def role_at(role, target):
    if target == "y":
        return role ^ 2
    if target in ("c", 3, -3):
        return role ^ 1
    return role


def arrivals():
    table = {role: {} for role in EDGES}
    for role, edges in EDGES.items():
        for number, (source, half, target, slot) in enumerate(edges):
            table[role_at(role, target)][slot] = (BACK[target], number, half)
    return table


ARRIVE = arrivals()


def place(target):
    me, count = lax.axis_index("row"), lax.axis_size("row")
    if target == "y":
        return me + 2 - 4 * (me // 2 % 2)
    if target == "c":
        return me + 1 - 2 * (me % 2)
    return (me + target + count) % count


def rows_of(slot, half, strip):
    if half == 0:
        return pl.ds(slot * strip, strip)
    return pl.ds(slot * strip + (half - 1) * (strip // 2), strip // 2)


def greet():
    me = lax.axis_index("row")
    barrier = pltpu.get_barrier_semaphore()
    for target in ("y", "c", 4, -4):
        pl.semaphore_signal(barrier, inc=1, device_id={"row": place(target)}, device_id_type=MESH)

    @pl.when(me % 2 == 0)
    def _():
        pl.semaphore_signal(barrier, inc=1, device_id={"row": place(-3)}, device_id_type=MESH)

    @pl.when(me % 2 == 1)
    def _():
        pl.semaphore_signal(barrier, inc=1, device_id={"row": place(3)}, device_id_type=MESH)

    pl.semaphore_wait(barrier, 5)


def gather_kernel(own_ref, out_ref, send_sem, recv_sem, keep_sem):
    planes, strip, _ = own_ref.shape
    greet()
    keep = pltpu.make_async_copy(own_ref, out_ref.at[:, pl.ds(OWN * strip, strip)], keep_sem)
    keep.start()

    def work(role):
        edges = EDGES[role]

        def edge(number, plane):
            source, half, target, slot = edges[number]
            if source == OWN:
                first = 0 if half < 2 else strip // 2
                origin = own_ref.at[plane, pl.ds(first, strip if half == 0 else strip // 2)]
            else:
                origin = out_ref.at[plane, rows_of(source, half, strip)]
            return pltpu.make_async_remote_copy(
                src_ref=origin,
                dst_ref=out_ref.at[plane, rows_of(slot, half, strip)],
                send_sem=send_sem.at[number, plane],
                recv_sem=recv_sem.at[slot, plane],
                device_id={"row": place(target)},
                device_id_type=MESH,
            )

        def arrived(slot, plane):
            back, _, half = ARRIVE[role][slot]
            spot = out_ref.at[plane, rows_of(slot, half, strip)]
            pltpu.make_async_remote_copy(
                src_ref=spot,
                dst_ref=spot,
                send_sem=send_sem.at[0, plane],
                recv_sem=recv_sem.at[slot, plane],
                device_id={"row": place(back)},
                device_id_type=MESH,
            ).wait_recv()

        near = P2 if role < 2 else M2
        far = {0: M1, 1: None, 2: P2, 3: P2}[role]

        def launch(source, plane):
            for number in range(len(edges)):
                if edges[number][0] == source:
                    edge(number, plane).start()

        for plane in range(planes):
            launch(OWN, plane)
        for step in range(planes + 1):
            if step < planes:
                arrived(near, step)
                launch(near, step)
            if step > 0 and far is not None:
                arrived(far, step - 1)
                launch(far, step - 1)
        for plane in range(planes):
            for slot in ARRIVE[role]:
                if slot not in (near, far):
                    arrived(slot, plane)
            for number in range(len(edges)):
                edge(number, plane).wait_send()

    me = lax.axis_index("row")
    for role in EDGES:
        pl.when(me % 4 == role)(functools.partial(work, role))
    keep.wait()


def scatter_kernel(grad_ref, out_ref, total, held, send_sem, recv_sem, load_sem):
    planes, strip = out_ref.shape[0], out_ref.shape[1]
    loads = [
        pltpu.make_async_copy(grad_ref.at[plane], total.at[plane], load_sem.at[plane])
        for plane in range(planes)
    ]
    for load in loads:
        load.start()
    greet()

    def work(role):
        edges = EDGES[role]
        slots = ARRIVE[role]

        def returned(slot, plane):
            target, number, half = slots[slot]
            count = strip if half == 0 else strip // 2
            return pltpu.make_async_remote_copy(
                src_ref=total.at[plane, rows_of(slot, half, strip)],
                dst_ref=held.at[number, plane, pl.ds(0, count)],
                send_sem=send_sem.at[slot, plane],
                recv_sem=recv_sem.at[number, plane],
                device_id={"row": place(target)},
                device_id_type=MESH,
            )

        def absorb(source, plane):
            for number, (origin, half, target, _) in enumerate(edges):
                if origin != source:
                    continue
                count = strip if half == 0 else strip // 2
                spot = held.at[number, plane, pl.ds(0, count)]
                pltpu.make_async_remote_copy(
                    src_ref=spot,
                    dst_ref=spot,
                    send_sem=send_sem.at[0, plane],
                    recv_sem=recv_sem.at[number, plane],
                    device_id={"row": place(target)},
                    device_id_type=MESH,
                ).wait_recv()
                rows = rows_of(source, half, strip)
                total[plane, rows] = total[plane, rows] + held[number, plane, pl.ds(0, count)]

        near = P2 if role < 2 else M2
        far = {0: M1, 1: None, 2: P2, 3: P2}[role]
        order = [slot for slot in (M2, P3, P1, M1) if slot in slots and slot not in (near, far)]
        for plane in range(planes):
            loads[plane].wait()
            for slot in order:
                returned(slot, plane).start()
        if far is not None:
            for plane in range(planes):
                absorb(far, plane)
                returned(far, plane).start()
        for plane in range(planes):
            absorb(near, plane)
            returned(near, plane).start()
        for plane in range(planes):
            absorb(OWN, plane)
            out_ref[plane] = total[plane, pl.ds(OWN * strip, strip)]
        for plane in range(planes):
            for slot in slots:
                returned(slot, plane).wait_send()

    me = lax.axis_index("row")
    for role in EDGES:
        pl.when(me % 4 == role)(functools.partial(work, role))


def extract_kernel(spot_ref, full_ref, out_ref):
    edge, columns = out_ref.shape[-1], full_ref.shape[-1]
    step = 64
    turn = (columns - spot_ref[1]) % columns
    past = spot_ref[0] % 8
    base = pl.multiple_of(spot_ref[0] - past, 8)

    @pl.loop(0, edge // step)
    def _(i):
        rows = full_ref[0, pl.ds(pl.multiple_of(base + i * step, 8), step + 8), :]
        rows = pltpu.roll(rows, (step + 8 - past) % (step + 8), 0)[:step]
        out_ref[0, pl.ds(i * step, step), :] = pltpu.roll(rows, turn, 1)[:, :edge]


def insert_kernel(spot_ref, grad_ref, out_ref, wide_ref):
    edge, columns = grad_ref.shape[-1], out_ref.shape[-1]
    step = 64
    past = spot_ref[0] % 8
    base = pl.multiple_of(spot_ref[0] - past, 8)
    out_ref[...] = jnp.zeros_like(out_ref)
    wide_ref[pl.ds(0, 8), :] = jnp.zeros((8, columns), jnp.float32)
    wide_ref[pl.ds(edge + 8, step), :] = jnp.zeros((step, columns), jnp.float32)

    @pl.loop(0, edge // step)
    def _(i):
        rows = grad_ref[0, pl.ds(i * step, step), :]
        wide = jnp.concatenate([rows, jnp.zeros((step, columns - edge), jnp.float32)], axis=1)
        wide_ref[pl.ds(i * step + 8, step), :] = pltpu.roll(wide, spot_ref[1], 1)

    @pl.loop(0, edge // step)
    def _(i):
        rows = wide_ref[pl.ds(i * step, step + 8), :]
        out_ref[0, pl.ds(pl.multiple_of(base + i * step, 8), step), :] = pltpu.roll(rows, step + past, 0)[:step]

    rows = wide_ref[pl.ds(edge, 16), :]
    out_ref[0, pl.ds(pl.multiple_of(base + edge, 8), 8), :] = pltpu.roll(rows, 8 + past, 0)[:8]


def gather(own, height):
    planes, strip, columns = own.shape
    return pl.pallas_call(
        gather_kernel,
        name="gather",
        out_shape=jax.ShapeDtypeStruct((planes, height, columns), jnp.float32),
        in_specs=[pl.BlockSpec(memory_space=pltpu.VMEM)],
        out_specs=pl.BlockSpec(memory_space=pl.ANY),
        scratch_shapes=[
            pltpu.SemaphoreType.DMA((MAX_EDGES, planes)),
            pltpu.SemaphoreType.DMA((6, planes)),
            pltpu.SemaphoreType.DMA,
        ],
        compiler_params=pltpu.CompilerParams(collective_id=0, has_side_effects=True),
    )(own)


def scatter(grads, strip):
    planes, height, columns = grads.shape
    return pl.pallas_call(
        scatter_kernel,
        name="scatter",
        out_shape=jax.ShapeDtypeStruct((planes, strip, columns), jnp.float32),
        in_specs=[pl.BlockSpec(memory_space=pl.ANY)],
        out_specs=pl.BlockSpec(memory_space=pltpu.VMEM),
        scratch_shapes=[
            pltpu.VMEM((planes, height, columns), jnp.float32),
            pltpu.VMEM((MAX_EDGES, planes, strip, columns), jnp.float32),
            pltpu.SemaphoreType.DMA((6, planes)),
            pltpu.SemaphoreType.DMA((MAX_EDGES, planes)),
            pltpu.SemaphoreType.DMA((planes,)),
        ],
        compiler_params=pltpu.CompilerParams(collective_id=1, has_side_effects=True),
    )(grads)


def local_move(kernel, name, spot, source, shape, scratch=()):
    planes = source.shape[0]
    return pl.pallas_call(
        kernel,
        name=name,
        out_shape=jax.ShapeDtypeStruct((planes, *shape), jnp.float32),
        grid_spec=pltpu.PrefetchScalarGridSpec(
            num_scalar_prefetch=1,
            grid=(planes,),
            in_specs=[pl.BlockSpec((1, *source.shape[1:]), lambda plane, spot: (plane, 0, 0))],
            out_specs=pl.BlockSpec((1, *shape), lambda plane, spot: (plane, 0, 0)),
            scratch_shapes=scratch,
        ),
    )(spot, source)


def dft_mats(length, flip):
    index = jnp.arange(length, dtype=jnp.int32)
    angles = (index[:, None] * index[None, :] % length).astype(jnp.float32) * (
        -2.0 * math.pi / length
    )
    factor = 1.0 / math.sqrt(length)
    cos_table = (jnp.cos(angles) * factor).astype(jnp.bfloat16)
    sin_table = (jnp.sin(angles) * factor).astype(jnp.bfloat16)
    if flip:
        sin_table = -sin_table
    left_real = jnp.concatenate([cos_table, -sin_table], axis=1)
    left_imag = jnp.concatenate([sin_table, cos_table], axis=1)
    right_real = jnp.concatenate([cos_table, -sin_table], axis=0)
    right_imag = jnp.concatenate([sin_table, cos_table], axis=0)
    return (left_real, left_imag, right_real, right_imag)


def transform(real_part, imag_part, mats):
    left_real, left_imag, right_real, right_imag = mats
    stacked = jnp.concatenate(
        [real_part.astype(jnp.bfloat16), imag_part.astype(jnp.bfloat16)], axis=0
    )
    half_real = jnp.dot(left_real, stacked, preferred_element_type=jnp.float32).astype(jnp.bfloat16)
    half_imag = jnp.dot(left_imag, stacked, preferred_element_type=jnp.float32).astype(jnp.bfloat16)
    joined = jnp.concatenate([half_real, half_imag], axis=1)
    return (
        jnp.dot(joined, right_real, preferred_element_type=jnp.float32),
        jnp.dot(joined, right_imag, preferred_element_type=jnp.float32),
    )


def cmul(a_real, a_imag, b_real, b_imag):
    return (a_real * b_real - a_imag * b_imag, a_real * b_imag + a_imag * b_real)


def cmul_conj(a_real, a_imag, b_real, b_imag):
    return (a_real * b_real + a_imag * b_imag, a_real * b_imag - a_imag * b_real)


def window_gradient(window, probe, amplitude, phase, forward, inverse):
    prop_real = jnp.cos(phase)
    prop_imag = jnp.sin(phase)
    probe_real, probe_imag = (probe[0], probe[1])
    first_real, first_imag = (window[0], window[1])
    second_real, second_imag = (window[2], window[3])
    exit_real, exit_imag = cmul(probe_real, probe_imag, first_real, first_imag)
    freq_real, freq_imag = transform(exit_real, exit_imag, forward)
    moved_real, moved_imag = cmul(freq_real, freq_imag, prop_real, prop_imag)
    inner_real, inner_imag = transform(moved_real, moved_imag, inverse)
    wave_real, wave_imag = cmul(inner_real, inner_imag, second_real, second_imag)
    far_real, far_imag = transform(wave_real, wave_imag, forward)
    modulus = jnp.sqrt(far_real * far_real + far_imag * far_imag)
    ratio = amplitude / jnp.maximum(modulus, 0.1)
    resid_real = far_real * (1.0 - ratio)
    resid_imag = far_imag * (1.0 - ratio)
    back_real, back_imag = transform(resid_real, resid_imag, inverse)
    grad2_real, grad2_imag = cmul_conj(inner_real, inner_imag, back_real, back_imag)
    mid_real, mid_imag = cmul_conj(second_real, second_imag, back_real, back_imag)
    spec_real, spec_imag = transform(mid_real, mid_imag, forward)
    unprop_real, unprop_imag = cmul_conj(prop_real, prop_imag, spec_real, spec_imag)
    entry_real, entry_imag = transform(unprop_real, unprop_imag, inverse)
    grad1_real, grad1_imag = cmul_conj(probe_real, probe_imag, entry_real, entry_imag)
    return jnp.stack([grad1_real, grad1_imag, grad2_real, grad2_imag])


def body(object_field, row_offset, col_offset, amplitudes, probe, phase):
    strip, columns = object_field.shape[2:]
    edge = probe.shape[1]
    half = strip // 2
    height = 5 * strip + half
    forward = dft_mats(edge, False)
    inverse = dft_mats(edge, True)
    own = object_field.reshape(4, strip, columns)
    spot = jnp.concatenate([row_offset + half, col_offset])
    around = gather(own, height)
    window = local_move(extract_kernel, "extract", spot, around, (edge, edge))
    grads = window_gradient(window, probe, amplitudes[0], phase, forward, inverse)
    spread = local_move(
        insert_kernel, "insert", spot, grads, (height, columns),
        [pltpu.VMEM((edge + 72, columns), jnp.float32)],
    )
    total = scatter(spread, strip)
    return (own - 0.5 * total).reshape(object_field.shape)


def solution(mesh):
    placed = (
        P(None, None, ("scan", "row"), None),
        P(("scan", "row")),
        P(("scan", "row")),
        P(("scan", "row"), None, None),
        P("scan", None, None),
        P(),
    )
    return jax.shard_map(
        body,
        mesh=mesh,
        in_specs=placed,
        out_specs=P(None, None, ("scan", "row"), None),
        check_vma=False,
    )
```

```python
import functools
import math

import jax
import jax.numpy as jnp
from jax import lax
from jax.experimental import pallas as pl
from jax.experimental.pallas import tpu as pltpu
from jax.sharding import PartitionSpec as P

MESH = pl.DeviceIdType.MESH

M2, M1, OWN, P1, P2, P3 = range(6)
EDGES = {
    0: (
        (OWN, 2, "y", M2), (OWN, 1, -3, P3), (OWN, 0, "c", M1),
        (P2, 2, 4, M2), (P2, 0, "c", P1), (M1, 2, "c", M2),
    ),
    1: (
        (OWN, 0, "y", M2), (OWN, 0, "c", P1),
        (P2, 0, 3, M1), (P2, 1, "c", P3), (P3, 1, "y", P1),
    ),
    2: (
        (OWN, 0, "y", P2), (OWN, 1, -3, P3), (OWN, 0, "c", M1),
        (M2, 2, -4, P2), (P2, 2, "c", P1),
    ),
    3: (
        (OWN, 0, "y", P2), (OWN, 0, "c", P1),
        (M2, 0, -4, P2), (M2, 0, "c", M1), (P2, 1, "c", P3), (P1, 1, "c", P2),
    ),
}
RELAYS = {
    0: ((P2, 0), (M1, 0)),
    1: ((P2, 0), (P3, 1)),
    2: ((M2, 2), (P2, 2)),
    3: ((M2, 0), (P1, 1), (P2, 0)),
}
COLUMN_PARTS = 2
BACK = {"y": "y", "c": "c", 3: -3, -3: 3, 4: -4, -4: 4}
MAX_EDGES = max(len(edges) for edges in EDGES.values())


def role_at(role, target):
    if target == "y":
        return role ^ 2
    if target in ("c", 3, -3):
        return role ^ 1
    return role


def arrivals():
    table = {role: {} for role in EDGES}
    for role, edges in EDGES.items():
        for number, (source, half, target, slot) in enumerate(edges):
            table[role_at(role, target)][slot, half] = (BACK[target], number)
    return table


ARRIVE = arrivals()


def place(target):
    me, count = lax.axis_index("row"), lax.axis_size("row")
    if target == "y":
        return me + 2 - 4 * (me // 2 % 2)
    if target == "c":
        return me + 1 - 2 * (me % 2)
    return (me + target + count) % count


def rows_of(slot, half, strip):
    if half == 0:
        return pl.ds(slot * strip, strip)
    return pl.ds(slot * strip + (half - 1) * (strip // 2), strip // 2)


def mark(key):
    return 2 * key[0] + (key[1] == 2)


def source_key(role, source, half):
    return (source, 0) if (source, 0) in ARRIVE[role] else (source, half)


def chunks_of(planes, columns):
    width = columns // COLUMN_PARTS
    return [(plane, pl.ds(part * width, width)) for plane in range(planes) for part in range(COLUMN_PARTS)]


def greet():
    me = lax.axis_index("row")
    barrier = pltpu.get_barrier_semaphore()
    for target in ("y", "c", 4, -4):
        pl.semaphore_signal(barrier, inc=1, device_id={"row": place(target)}, device_id_type=MESH)

    @pl.when(me % 2 == 0)
    def _():
        pl.semaphore_signal(barrier, inc=1, device_id={"row": place(-3)}, device_id_type=MESH)

    @pl.when(me % 2 == 1)
    def _():
        pl.semaphore_signal(barrier, inc=1, device_id={"row": place(3)}, device_id_type=MESH)

    pl.semaphore_wait(barrier, 5)


def gather_kernel(own_ref, out_ref, send_sem, recv_sem, keep_sem):
    planes, strip, columns = own_ref.shape
    chunks = chunks_of(planes, columns)
    greet()
    keep = pltpu.make_async_copy(own_ref, out_ref.at[:, pl.ds(OWN * strip, strip)], keep_sem)
    keep.start()

    def work(role):
        edges = EDGES[role]

        def edge(number, chunk):
            source, half, target, slot = edges[number]
            plane, lanes = chunks[chunk]
            if source == OWN:
                origin = own_ref.at[plane, rows_of(0, half, strip), lanes]
            else:
                origin = out_ref.at[plane, rows_of(source, half, strip), lanes]
            return pltpu.make_async_remote_copy(
                src_ref=origin,
                dst_ref=out_ref.at[plane, rows_of(slot, half, strip), lanes],
                send_sem=send_sem.at[number, chunk],
                recv_sem=recv_sem.at[mark((slot, half)), chunk],
                device_id={"row": place(target)},
                device_id_type=MESH,
            )

        def arrived(key, chunk):
            back, _ = ARRIVE[role][key]
            plane, lanes = chunks[chunk]
            spot = out_ref.at[plane, rows_of(*key, strip), lanes]
            pltpu.make_async_remote_copy(
                src_ref=spot,
                dst_ref=spot,
                send_sem=send_sem.at[0, chunk],
                recv_sem=recv_sem.at[mark(key), chunk],
                device_id={"row": place(back)},
                device_id_type=MESH,
            ).wait_recv()

        def launch(key, chunk):
            for number, (source, half, _, _) in enumerate(edges):
                if (source == OWN) if key is None else (source != OWN and source_key(role, source, half) == key):
                    edge(number, chunk).start()

        for chunk in range(len(chunks)):
            launch(None, chunk)
        relays = RELAYS[role]
        for step in range(len(chunks) + len(relays) - 1):
            for late, key in enumerate(relays):
                if 0 <= step - late < len(chunks):
                    arrived(key, step - late)
                    launch(key, step - late)
        for chunk in range(len(chunks)):
            for key in ARRIVE[role]:
                if key not in relays:
                    arrived(key, chunk)
            for number in range(len(edges)):
                edge(number, chunk).wait_send()

    me = lax.axis_index("row")
    for role in EDGES:
        pl.when(me % 4 == role)(functools.partial(work, role))
    keep.wait()


def scatter_kernel(grad_ref, out_ref, total, held, send_sem, recv_sem, load_sem):
    planes, strip, columns = out_ref.shape
    chunks = chunks_of(planes, columns)
    loads = [
        pltpu.make_async_copy(grad_ref.at[plane], total.at[plane], load_sem.at[plane])
        for plane in range(planes)
    ]
    for load in loads:
        load.start()
    greet()

    def work(role):
        edges = EDGES[role]
        keys = ARRIVE[role]

        def returned(key, chunk):
            target, number = keys[key]
            plane, lanes = chunks[chunk]
            count = strip if key[1] == 0 else strip // 2
            return pltpu.make_async_remote_copy(
                src_ref=total.at[plane, rows_of(*key, strip), lanes],
                dst_ref=held.at[number, plane, pl.ds(0, count), lanes],
                send_sem=send_sem.at[mark(key), chunk],
                recv_sem=recv_sem.at[number, chunk],
                device_id={"row": place(target)},
                device_id_type=MESH,
            )

        def absorb(key, chunk):
            plane, lanes = chunks[chunk]
            for number, (source, half, target, _) in enumerate(edges):
                if not ((source == OWN) if key is None else (source != OWN and source_key(role, source, half) == key)):
                    continue
                count = strip if half == 0 else strip // 2
                spot = held.at[number, plane, pl.ds(0, count), lanes]
                pltpu.make_async_remote_copy(
                    src_ref=spot,
                    dst_ref=spot,
                    send_sem=send_sem.at[0, chunk],
                    recv_sem=recv_sem.at[number, chunk],
                    device_id={"row": place(target)},
                    device_id_type=MESH,
                ).wait_recv()
                rows = rows_of(source, half, strip)
                total[plane, rows, lanes] = total[plane, rows, lanes] + held[number, plane, pl.ds(0, count), lanes]

        relays = RELAYS[role][::-1]
        order = [key for key in keys if key not in relays]
        order.sort(key=lambda key: (keys[key][0] == "c" and key[0] == M1, key[0]))
        for chunk in range(len(chunks)):
            if chunk % COLUMN_PARTS == 0:
                loads[chunks[chunk][0]].wait()
            for key in order:
                returned(key, chunk).start()
        for step in range(len(chunks) + len(relays) - 1):
            for late, key in enumerate(relays):
                if 0 <= step - late < len(chunks):
                    absorb(key, step - late)
                    returned(key, step - late).start()
        for chunk in range(len(chunks)):
            plane, lanes = chunks[chunk]
            absorb(None, chunk)
            out_ref[plane, :, lanes] = total[plane, pl.ds(OWN * strip, strip), lanes]
        for chunk in range(len(chunks)):
            for key in keys:
                returned(key, chunk).wait_send()

    me = lax.axis_index("row")
    for role in EDGES:
        pl.when(me % 4 == role)(functools.partial(work, role))


def extract_kernel(spot_ref, full_ref, out_ref):
    edge, columns = out_ref.shape[-1], full_ref.shape[-1]
    step = 64
    turn = (columns - spot_ref[1]) % columns
    past = spot_ref[0] % 8
    base = pl.multiple_of(spot_ref[0] - past, 8)

    @pl.loop(0, edge // step)
    def _(i):
        rows = full_ref[0, pl.ds(pl.multiple_of(base + i * step, 8), step + 8), :]
        rows = pltpu.roll(rows, (step + 8 - past) % (step + 8), 0)[:step]
        out_ref[0, pl.ds(i * step, step), :] = pltpu.roll(rows, turn, 1)[:, :edge]


def insert_kernel(spot_ref, grad_ref, out_ref, wide_ref):
    edge, columns = grad_ref.shape[-1], out_ref.shape[-1]
    step = 64
    past = spot_ref[0] % 8
    base = pl.multiple_of(spot_ref[0] - past, 8)
    out_ref[...] = jnp.zeros_like(out_ref)
    wide_ref[pl.ds(0, 8), :] = jnp.zeros((8, columns), jnp.float32)
    wide_ref[pl.ds(edge + 8, step), :] = jnp.zeros((step, columns), jnp.float32)

    @pl.loop(0, edge // step)
    def _(i):
        rows = grad_ref[0, pl.ds(i * step, step), :]
        wide = jnp.concatenate([rows, jnp.zeros((step, columns - edge), jnp.float32)], axis=1)
        wide_ref[pl.ds(i * step + 8, step), :] = pltpu.roll(wide, spot_ref[1], 1)

    @pl.loop(0, edge // step)
    def _(i):
        rows = wide_ref[pl.ds(i * step, step + 8), :]
        out_ref[0, pl.ds(pl.multiple_of(base + i * step, 8), step), :] = pltpu.roll(rows, step + past, 0)[:step]

    rows = wide_ref[pl.ds(edge, 16), :]
    out_ref[0, pl.ds(pl.multiple_of(base + edge, 8), 8), :] = pltpu.roll(rows, 8 + past, 0)[:8]


def gather(own, height):
    planes, strip, columns = own.shape
    return pl.pallas_call(
        gather_kernel,
        name="gather",
        out_shape=jax.ShapeDtypeStruct((planes, height, columns), jnp.float32),
        in_specs=[pl.BlockSpec(memory_space=pltpu.VMEM)],
        out_specs=pl.BlockSpec(memory_space=pl.ANY),
        scratch_shapes=[
            pltpu.SemaphoreType.DMA((MAX_EDGES, planes * COLUMN_PARTS)),
            pltpu.SemaphoreType.DMA((12, planes * COLUMN_PARTS)),
            pltpu.SemaphoreType.DMA,
        ],
        compiler_params=pltpu.CompilerParams(collective_id=0, has_side_effects=True),
    )(own)


def scatter(grads, strip):
    planes, height, columns = grads.shape
    return pl.pallas_call(
        scatter_kernel,
        name="scatter",
        out_shape=jax.ShapeDtypeStruct((planes, strip, columns), jnp.float32),
        in_specs=[pl.BlockSpec(memory_space=pl.ANY)],
        out_specs=pl.BlockSpec(memory_space=pltpu.VMEM),
        scratch_shapes=[
            pltpu.VMEM((planes, height, columns), jnp.float32),
            pltpu.VMEM((MAX_EDGES, planes, strip, columns), jnp.float32),
            pltpu.SemaphoreType.DMA((12, planes * COLUMN_PARTS)),
            pltpu.SemaphoreType.DMA((MAX_EDGES, planes * COLUMN_PARTS)),
            pltpu.SemaphoreType.DMA((planes,)),
        ],
        compiler_params=pltpu.CompilerParams(collective_id=1, has_side_effects=True),
    )(grads)


def local_move(kernel, name, spot, source, shape, scratch=()):
    planes = source.shape[0]
    return pl.pallas_call(
        kernel,
        name=name,
        out_shape=jax.ShapeDtypeStruct((planes, *shape), jnp.float32),
        grid_spec=pltpu.PrefetchScalarGridSpec(
            num_scalar_prefetch=1,
            grid=(planes,),
            in_specs=[pl.BlockSpec((1, *source.shape[1:]), lambda plane, spot: (plane, 0, 0))],
            out_specs=pl.BlockSpec((1, *shape), lambda plane, spot: (plane, 0, 0)),
            scratch_shapes=scratch,
        ),
    )(spot, source)


def dft_mats(length, flip):
    index = jnp.arange(length, dtype=jnp.int32)
    angles = (index[:, None] * index[None, :] % length).astype(jnp.float32) * (
        -2.0 * math.pi / length
    )
    factor = 1.0 / math.sqrt(length)
    cos_table = (jnp.cos(angles) * factor).astype(jnp.bfloat16)
    sin_table = (jnp.sin(angles) * factor).astype(jnp.bfloat16)
    if flip:
        sin_table = -sin_table
    left_real = jnp.concatenate([cos_table, -sin_table], axis=1)
    left_imag = jnp.concatenate([sin_table, cos_table], axis=1)
    right_real = jnp.concatenate([cos_table, -sin_table], axis=0)
    right_imag = jnp.concatenate([sin_table, cos_table], axis=0)
    return (left_real, left_imag, right_real, right_imag)


def transform(real_part, imag_part, mats):
    left_real, left_imag, right_real, right_imag = mats
    stacked = jnp.concatenate(
        [real_part.astype(jnp.bfloat16), imag_part.astype(jnp.bfloat16)], axis=0
    )
    half_real = jnp.dot(left_real, stacked, preferred_element_type=jnp.float32).astype(jnp.bfloat16)
    half_imag = jnp.dot(left_imag, stacked, preferred_element_type=jnp.float32).astype(jnp.bfloat16)
    joined = jnp.concatenate([half_real, half_imag], axis=1)
    return (
        jnp.dot(joined, right_real, preferred_element_type=jnp.float32),
        jnp.dot(joined, right_imag, preferred_element_type=jnp.float32),
    )


def cmul(a_real, a_imag, b_real, b_imag):
    return (a_real * b_real - a_imag * b_imag, a_real * b_imag + a_imag * b_real)


def cmul_conj(a_real, a_imag, b_real, b_imag):
    return (a_real * b_real + a_imag * b_imag, a_real * b_imag - a_imag * b_real)


def window_gradient(window, probe, amplitude, phase, forward, inverse):
    prop_real = jnp.cos(phase)
    prop_imag = jnp.sin(phase)
    probe_real, probe_imag = (probe[0], probe[1])
    first_real, first_imag = (window[0], window[1])
    second_real, second_imag = (window[2], window[3])
    exit_real, exit_imag = cmul(probe_real, probe_imag, first_real, first_imag)
    freq_real, freq_imag = transform(exit_real, exit_imag, forward)
    moved_real, moved_imag = cmul(freq_real, freq_imag, prop_real, prop_imag)
    inner_real, inner_imag = transform(moved_real, moved_imag, inverse)
    wave_real, wave_imag = cmul(inner_real, inner_imag, second_real, second_imag)
    far_real, far_imag = transform(wave_real, wave_imag, forward)
    modulus = jnp.sqrt(far_real * far_real + far_imag * far_imag)
    ratio = amplitude / jnp.maximum(modulus, 0.1)
    resid_real = far_real * (1.0 - ratio)
    resid_imag = far_imag * (1.0 - ratio)
    back_real, back_imag = transform(resid_real, resid_imag, inverse)
    grad2_real, grad2_imag = cmul_conj(inner_real, inner_imag, back_real, back_imag)
    mid_real, mid_imag = cmul_conj(second_real, second_imag, back_real, back_imag)
    spec_real, spec_imag = transform(mid_real, mid_imag, forward)
    unprop_real, unprop_imag = cmul_conj(prop_real, prop_imag, spec_real, spec_imag)
    entry_real, entry_imag = transform(unprop_real, unprop_imag, inverse)
    grad1_real, grad1_imag = cmul_conj(probe_real, probe_imag, entry_real, entry_imag)
    return jnp.stack([grad1_real, grad1_imag, grad2_real, grad2_imag])


def body(object_field, row_offset, col_offset, amplitudes, probe, phase):
    strip, columns = object_field.shape[2:]
    edge = probe.shape[1]
    half = strip // 2
    height = 5 * strip + half
    forward = dft_mats(edge, False)
    inverse = dft_mats(edge, True)
    own = object_field.reshape(4, strip, columns)
    spot = jnp.concatenate([row_offset + half, col_offset])
    around = gather(own, height)
    window = local_move(extract_kernel, "extract", spot, around, (edge, edge))
    grads = window_gradient(window, probe, amplitudes[0], phase, forward, inverse)
    spread = local_move(
        insert_kernel, "insert", spot, grads, (height, columns),
        [pltpu.VMEM((edge + 72, columns), jnp.float32)],
    )
    total = scatter(spread, strip)
    return (own - 0.5 * total).reshape(object_field.shape)


def solution(mesh):
    placed = (
        P(None, None, ("scan", "row"), None),
        P(("scan", "row")),
        P(("scan", "row")),
        P(("scan", "row"), None, None),
        P("scan", None, None),
        P(),
    )
    return jax.shard_map(
        body,
        mesh=mesh,
        in_specs=placed,
        out_specs=P(None, None, ("scan", "row"), None),
        check_vma=False,
    )
```

```python
import functools
import math

import jax
import jax.numpy as jnp
from jax import lax
from jax.experimental import pallas as pl
from jax.experimental.pallas import tpu as pltpu
from jax.sharding import PartitionSpec as P

MESH = pl.DeviceIdType.MESH

M2, M1, OWN, P1, P2, P3 = range(6)
EDGES = {
    0: (
        (OWN, 2, "y", M2), (OWN, 1, -3, P3), (OWN, 0, "c", M1),
        (P2, 2, 4, M2), (P2, 0, "c", P1), (M1, 2, "c", M2),
    ),
    1: (
        (OWN, 0, "y", M2), (OWN, 0, "c", P1),
        (P2, 0, 3, M1), (P2, 1, "c", P3), (P3, 1, "y", P1),
    ),
    2: (
        (OWN, 0, "y", P2), (OWN, 1, -3, P3), (OWN, 0, "c", M1),
        (M2, 2, -4, P2), (P2, 2, "c", P1),
    ),
    3: (
        (OWN, 0, "y", P2), (OWN, 0, "c", P1),
        (M2, 0, -4, P2), (M2, 0, "c", M1), (P2, 1, "c", P3), (P1, 1, "c", P2),
    ),
}
RELAYS = {
    0: ((P2, 0), (M1, 0)),
    1: ((P2, 0), (P3, 1)),
    2: ((M2, 2), (P2, 2)),
    3: ((M2, 0), (P1, 1), (P2, 0)),
}
COLUMN_PARTS = 2
BACK = {"y": "y", "c": "c", 3: -3, -3: 3, 4: -4, -4: 4}
MAX_EDGES = max(len(edges) for edges in EDGES.values())


def role_at(role, target):
    if target == "y":
        return role ^ 2
    if target in ("c", 3, -3):
        return role ^ 1
    return role


def arrivals():
    table = {role: {} for role in EDGES}
    for role, edges in EDGES.items():
        for number, (source, half, target, slot) in enumerate(edges):
            table[role_at(role, target)][slot, half] = (BACK[target], number)
    return table


ARRIVE = arrivals()


def place(target):
    me, count = lax.axis_index("row"), lax.axis_size("row")
    if target == "y":
        return me + 2 - 4 * (me // 2 % 2)
    if target == "c":
        return me + 1 - 2 * (me % 2)
    return (me + target + count) % count


def rows_of(slot, half, strip):
    if half == 0:
        return pl.ds(slot * strip, strip)
    return pl.ds(slot * strip + (half - 1) * (strip // 2), strip // 2)


def mark(key):
    return 2 * key[0] + (key[1] == 2)


def source_key(role, source, half):
    return (source, 0) if (source, 0) in ARRIVE[role] else (source, half)


def chunks_of(planes, columns):
    width = columns // COLUMN_PARTS
    return [(plane, pl.ds(part * width, width)) for plane in range(planes) for part in range(COLUMN_PARTS)]


def greet():
    me = lax.axis_index("row")
    barrier = pltpu.get_barrier_semaphore()
    for target in ("y", "c", 4, -4):
        pl.semaphore_signal(barrier, inc=1, device_id={"row": place(target)}, device_id_type=MESH)

    @pl.when(me % 2 == 0)
    def _():
        pl.semaphore_signal(barrier, inc=1, device_id={"row": place(-3)}, device_id_type=MESH)

    @pl.when(me % 2 == 1)
    def _():
        pl.semaphore_signal(barrier, inc=1, device_id={"row": place(3)}, device_id_type=MESH)

    pl.semaphore_wait(barrier, 5)


def table_rows(first, count, phase_ref, tables):
    fore_left_real, fore_left_imag, fore_right_real, fore_right_imag = tables[0:4]
    back_left_real, back_left_imag, back_right_real, back_right_imag = tables[4:8]
    prop_real, prop_imag = tables[8:10]
    edge = phase_ref.shape[0]
    step = 16

    @pl.loop(0, count // step)
    def _(i):
        start = pl.multiple_of(first + i * step, step)
        rows, low, high = pl.ds(start, step), pl.ds(0, edge), pl.ds(edge, edge)
        more = pl.ds(pl.multiple_of(edge + start, step), step)
        line = lax.broadcasted_iota(jnp.int32, (step, edge), 0) + start
        index = line * lax.broadcasted_iota(jnp.int32, (step, edge), 1)
        wrapped = index & (edge - 1) if edge & (edge - 1) == 0 else lax.rem(index, edge)
        angles = wrapped.astype(jnp.float32) * (-2.0 * math.pi / edge)
        factor = 1.0 / math.sqrt(edge)
        cosine = (jnp.cos(angles) * factor).astype(jnp.bfloat16)
        plain = jnp.sin(angles) * factor
        sine, minus = plain.astype(jnp.bfloat16), (-plain).astype(jnp.bfloat16)
        fore_left_real[rows, low] = cosine
        fore_left_real[rows, high] = minus
        fore_left_imag[rows, low] = sine
        fore_left_imag[rows, high] = cosine
        fore_right_real[rows, :] = cosine
        fore_right_real[more, :] = minus
        fore_right_imag[rows, :] = sine
        fore_right_imag[more, :] = cosine
        back_left_real[rows, low] = cosine
        back_left_real[rows, high] = sine
        back_left_imag[rows, low] = minus
        back_left_imag[rows, high] = cosine
        back_right_real[rows, :] = cosine
        back_right_real[more, :] = sine
        back_right_imag[rows, :] = minus
        back_right_imag[more, :] = cosine
        prop_real[rows, :] = jnp.cos(phase_ref[rows, :])
        prop_imag[rows, :] = jnp.sin(phase_ref[rows, :])


def feeds(role, edge, key):
    source, half = edge[0], edge[1]
    if key is None:
        return source == OWN
    return source != OWN and source_key(role, source, half) == key


def gather_kernel(own_ref, phase_ref, out_ref, *refs):
    tables = refs[:10]
    send_sem, recv_sem, keep_sem = refs[10:]
    full = [out_ref.at[plane] for plane in range(own_ref.shape[0])]
    planes, strip, columns = own_ref.shape
    chunks = chunks_of(planes, columns)
    me = lax.axis_index("row")
    greet()

    def edge(role, number, chunk):
        source, half, target, slot = EDGES[role][number]
        plane, lanes = chunks[chunk]
        if source == OWN:
            origin = own_ref.at[plane, rows_of(0, half, strip), lanes]
        else:
            origin = full[plane].at[rows_of(source, half, strip), lanes]
        return pltpu.make_async_remote_copy(
            src_ref=origin,
            dst_ref=full[plane].at[rows_of(slot, half, strip), lanes],
            send_sem=send_sem.at[number, chunk],
            recv_sem=recv_sem.at[mark((slot, half)), chunk],
            device_id={"row": place(target)},
            device_id_type=MESH,
        )

    def arrived(role, key, chunk):
        back, _ = ARRIVE[role][key]
        plane, lanes = chunks[chunk]
        spot = full[plane].at[rows_of(*key, strip), lanes]
        pltpu.make_async_remote_copy(
            src_ref=spot,
            dst_ref=spot,
            send_sem=send_sem.at[0, chunk],
            recv_sem=recv_sem.at[mark(key), chunk],
            device_id={"row": place(back)},
            device_id_type=MESH,
        ).wait_recv()

    def launch(role, key, chunk):
        for number, entry in enumerate(EDGES[role]):
            if feeds(role, entry, key):
                edge(role, number, chunk).start()

    def begin(role):
        for chunk in range(len(chunks)):
            launch(role, None, chunk)

    def relay(role, step):
        for late, key in enumerate(RELAYS[role]):
            if 0 <= step - late < len(chunks):
                arrived(role, key, step - late)
                launch(role, key, step - late)

    def rest(role, plane):
        for chunk in range(plane * COLUMN_PARTS, (plane + 1) * COLUMN_PARTS):
            for key in ARRIVE[role]:
                if key not in RELAYS[role]:
                    arrived(role, key, chunk)

    def drain(role):
        for chunk in range(len(chunks)):
            for number in range(len(EDGES[role])):
                edge(role, number, chunk).wait_send()

    def by_role(work, *args):
        for role in EDGES:
            pl.when(me % 4 == role)(functools.partial(work, role, *args))

    by_role(begin)
    keeps = [
        pltpu.make_async_copy(
            own_ref.at[plane], full[plane].at[pl.ds(OWN * strip, strip)], keep_sem.at[plane]
        )
        for plane in range(planes)
    ]
    for keep in keeps:
        keep.start()
    share = phase_ref.shape[0] // len(chunks)
    late = max(len(relays) for relays in RELAYS.values()) - 1
    for step in range(len(chunks) + late):
        if step < len(chunks):
            table_rows(step * share, share, phase_ref, tables)
        by_role(relay, step)
    for plane in range(planes):
        by_role(rest, plane)
        keeps[plane].wait()
    by_role(drain)


def scatter_kernel(grad_ref, out_ref, total, held, send_sem, recv_sem, load_sem):
    planes, strip, columns = out_ref.shape
    chunks = chunks_of(planes, columns)
    loads = [
        pltpu.make_async_copy(grad_ref.at[plane], total.at[plane], load_sem.at[plane])
        for plane in range(planes)
    ]
    for load in loads:
        load.start()
    greet()

    def work(role):
        edges = EDGES[role]
        keys = ARRIVE[role]

        def returned(key, chunk):
            target, number = keys[key]
            plane, lanes = chunks[chunk]
            count = strip if key[1] == 0 else strip // 2
            return pltpu.make_async_remote_copy(
                src_ref=total.at[plane, rows_of(*key, strip), lanes],
                dst_ref=held.at[number, plane, pl.ds(0, count), lanes],
                send_sem=send_sem.at[mark(key), chunk],
                recv_sem=recv_sem.at[number, chunk],
                device_id={"row": place(target)},
                device_id_type=MESH,
            )

        def absorb(key, chunk):
            plane, lanes = chunks[chunk]
            for number, (source, half, target, _) in enumerate(edges):
                if not feeds(role, (source, half), key):
                    continue
                count = strip if half == 0 else strip // 2
                spot = held.at[number, plane, pl.ds(0, count), lanes]
                pltpu.make_async_remote_copy(
                    src_ref=spot,
                    dst_ref=spot,
                    send_sem=send_sem.at[0, chunk],
                    recv_sem=recv_sem.at[number, chunk],
                    device_id={"row": place(target)},
                    device_id_type=MESH,
                ).wait_recv()
                rows = rows_of(source, half, strip)
                total[plane, rows, lanes] = total[plane, rows, lanes] + held[number, plane, pl.ds(0, count), lanes]

        relays = RELAYS[role][::-1]
        order = [key for key in keys if key not in relays]
        order.sort(key=lambda key: (keys[key][0] == "c" and key[0] == M1, key[0]))
        for chunk in range(len(chunks)):
            if chunk % COLUMN_PARTS == 0:
                loads[chunks[chunk][0]].wait()
            for key in order:
                returned(key, chunk).start()
        for step in range(len(chunks) + len(relays) - 1):
            for late, key in enumerate(relays):
                if 0 <= step - late < len(chunks):
                    absorb(key, step - late)
                    returned(key, step - late).start()
        for chunk in range(len(chunks)):
            plane, lanes = chunks[chunk]
            absorb(None, chunk)
            out_ref[plane, :, lanes] = total[plane, pl.ds(OWN * strip, strip), lanes]
        for chunk in range(len(chunks)):
            for key in keys:
                returned(key, chunk).wait_send()

    me = lax.axis_index("row")
    for role in EDGES:
        pl.when(me % 4 == role)(functools.partial(work, role))


def extract_kernel(spot_ref, full_ref, out_ref):
    edge, columns = out_ref.shape[-1], full_ref.shape[-1]
    step = 64
    turn = (columns - spot_ref[1]) % columns
    past = spot_ref[0] % 8
    base = pl.multiple_of(spot_ref[0] - past, 8)

    @pl.loop(0, edge // step)
    def _(i):
        rows = full_ref[0, pl.ds(pl.multiple_of(base + i * step, 8), step + 8), :]
        rows = pltpu.roll(rows, (step + 8 - past) % (step + 8), 0)[:step]
        out_ref[0, pl.ds(i * step, step), :] = pltpu.roll(rows, turn, 1)[:, :edge]


def insert_kernel(spot_ref, grad_ref, out_ref, wide_ref):
    edge, columns = grad_ref.shape[-1], out_ref.shape[-1]
    step = 64
    past = spot_ref[0] % 8
    base = pl.multiple_of(spot_ref[0] - past, 8)
    out_ref[...] = jnp.zeros_like(out_ref)
    wide_ref[pl.ds(0, 8), :] = jnp.zeros((8, columns), jnp.float32)
    wide_ref[pl.ds(edge + 8, step), :] = jnp.zeros((step, columns), jnp.float32)

    @pl.loop(0, edge // step)
    def _(i):
        rows = grad_ref[0, pl.ds(i * step, step), :]
        wide = jnp.concatenate([rows, jnp.zeros((step, columns - edge), jnp.float32)], axis=1)
        wide_ref[pl.ds(i * step + 8, step), :] = pltpu.roll(wide, spot_ref[1], 1)

    @pl.loop(0, edge // step)
    def _(i):
        rows = wide_ref[pl.ds(i * step, step + 8), :]
        out_ref[0, pl.ds(pl.multiple_of(base + i * step, 8), step), :] = pltpu.roll(rows, step + past, 0)[:step]

    rows = wide_ref[pl.ds(edge, 16), :]
    out_ref[0, pl.ds(pl.multiple_of(base + edge, 8), 8), :] = pltpu.roll(rows, 8 + past, 0)[:8]


def gather(own, phase, height):
    planes, strip, columns = own.shape
    edge = phase.shape[0]
    left = jax.ShapeDtypeStruct((edge, 2 * edge), jnp.bfloat16)
    right = jax.ShapeDtypeStruct((2 * edge, edge), jnp.bfloat16)
    flat = jax.ShapeDtypeStruct((edge, edge), jnp.float32)
    vmem = pl.BlockSpec(memory_space=pltpu.VMEM)
    parts = planes * COLUMN_PARTS
    return pl.pallas_call(
        gather_kernel,
        name="gather",
        out_shape=[
            jax.ShapeDtypeStruct((planes, height, columns), jnp.float32),
            left, left, right, right, left, left, right, right, flat, flat,
        ],
        in_specs=[vmem, vmem],
        out_specs=[pl.BlockSpec(memory_space=pl.ANY)] + [vmem] * 10,
        scratch_shapes=[
            pltpu.SemaphoreType.DMA((MAX_EDGES, parts)),
            pltpu.SemaphoreType.DMA((12, parts)),
            pltpu.SemaphoreType.DMA((planes,)),
        ],
        compiler_params=pltpu.CompilerParams(collective_id=0, has_side_effects=True),
    )(own, phase)


def scatter(grads, strip):
    planes, height, columns = grads.shape
    return pl.pallas_call(
        scatter_kernel,
        name="scatter",
        out_shape=jax.ShapeDtypeStruct((planes, strip, columns), jnp.float32),
        in_specs=[pl.BlockSpec(memory_space=pl.ANY)],
        out_specs=pl.BlockSpec(memory_space=pltpu.VMEM),
        scratch_shapes=[
            pltpu.VMEM((planes, height, columns), jnp.float32),
            pltpu.VMEM((MAX_EDGES, planes, strip, columns), jnp.float32),
            pltpu.SemaphoreType.DMA((12, planes * COLUMN_PARTS)),
            pltpu.SemaphoreType.DMA((MAX_EDGES, planes * COLUMN_PARTS)),
            pltpu.SemaphoreType.DMA((planes,)),
        ],
        compiler_params=pltpu.CompilerParams(collective_id=1, has_side_effects=True),
    )(grads)


def local_move(kernel, name, spot, source, shape, scratch=()):
    planes = source.shape[0]
    return pl.pallas_call(
        kernel,
        name=name,
        out_shape=jax.ShapeDtypeStruct((planes, *shape), jnp.float32),
        grid_spec=pltpu.PrefetchScalarGridSpec(
            num_scalar_prefetch=1,
            grid=(planes,),
            in_specs=[pl.BlockSpec((1, *source.shape[1:]), lambda plane, spot: (plane, 0, 0))],
            out_specs=pl.BlockSpec((1, *shape), lambda plane, spot: (plane, 0, 0)),
            scratch_shapes=scratch,
        ),
    )(spot, source)


def transform(real_part, imag_part, mats):
    left_real, left_imag, right_real, right_imag = mats
    stacked = jnp.concatenate(
        [real_part.astype(jnp.bfloat16), imag_part.astype(jnp.bfloat16)], axis=0
    )
    half_real = jnp.dot(left_real, stacked, preferred_element_type=jnp.float32).astype(jnp.bfloat16)
    half_imag = jnp.dot(left_imag, stacked, preferred_element_type=jnp.float32).astype(jnp.bfloat16)
    joined = jnp.concatenate([half_real, half_imag], axis=1)
    return (
        jnp.dot(joined, right_real, preferred_element_type=jnp.float32),
        jnp.dot(joined, right_imag, preferred_element_type=jnp.float32),
    )


def cmul(a_real, a_imag, b_real, b_imag):
    return (a_real * b_real - a_imag * b_imag, a_real * b_imag + a_imag * b_real)


def cmul_conj(a_real, a_imag, b_real, b_imag):
    return (a_real * b_real + a_imag * b_imag, a_real * b_imag - a_imag * b_real)


def window_gradient(window, probe, amplitude, propagator, forward, inverse):
    prop_real, prop_imag = propagator
    probe_real, probe_imag = (probe[0], probe[1])
    first_real, first_imag = (window[0], window[1])
    second_real, second_imag = (window[2], window[3])
    exit_real, exit_imag = cmul(probe_real, probe_imag, first_real, first_imag)
    freq_real, freq_imag = transform(exit_real, exit_imag, forward)
    moved_real, moved_imag = cmul(freq_real, freq_imag, prop_real, prop_imag)
    inner_real, inner_imag = transform(moved_real, moved_imag, inverse)
    wave_real, wave_imag = cmul(inner_real, inner_imag, second_real, second_imag)
    far_real, far_imag = transform(wave_real, wave_imag, forward)
    modulus = jnp.sqrt(far_real * far_real + far_imag * far_imag)
    ratio = amplitude / jnp.maximum(modulus, 0.1)
    resid_real = far_real * (1.0 - ratio)
    resid_imag = far_imag * (1.0 - ratio)
    back_real, back_imag = transform(resid_real, resid_imag, inverse)
    grad2_real, grad2_imag = cmul_conj(inner_real, inner_imag, back_real, back_imag)
    mid_real, mid_imag = cmul_conj(second_real, second_imag, back_real, back_imag)
    spec_real, spec_imag = transform(mid_real, mid_imag, forward)
    unprop_real, unprop_imag = cmul_conj(prop_real, prop_imag, spec_real, spec_imag)
    entry_real, entry_imag = transform(unprop_real, unprop_imag, inverse)
    grad1_real, grad1_imag = cmul_conj(probe_real, probe_imag, entry_real, entry_imag)
    return jnp.stack([grad1_real, grad1_imag, grad2_real, grad2_imag])


def body(object_field, row_offset, col_offset, amplitudes, probe, phase):
    strip, columns = object_field.shape[2:]
    edge = probe.shape[1]
    half = strip // 2
    height = 5 * strip + half
    own = object_field.reshape(4, strip, columns)
    spot = jnp.concatenate([row_offset + half, col_offset])
    around, *tables = gather(own, phase, height)
    forward, inverse, propagator = tables[:4], tables[4:8], tables[8:]
    window = local_move(extract_kernel, "extract", spot, around, (edge, edge))
    grads = window_gradient(window, probe, amplitudes[0], propagator, forward, inverse)
    spread = local_move(
        insert_kernel, "insert", spot, grads, (height, columns),
        [pltpu.VMEM((edge + 72, columns), jnp.float32)],
    )
    total = scatter(spread, strip)
    return (own - 0.5 * total).reshape(object_field.shape)


def solution(mesh):
    placed = (
        P(None, None, ("scan", "row"), None),
        P(("scan", "row")),
        P(("scan", "row")),
        P(("scan", "row"), None, None),
        P("scan", None, None),
        P(),
    )
    return jax.shard_map(
        body,
        mesh=mesh,
        in_specs=placed,
        out_specs=P(None, None, ("scan", "row"), None),
        check_vma=False,
    )
```

```python
import functools
import math

import jax
import jax.numpy as jnp
from jax import lax
from jax.experimental import pallas as pl
from jax.experimental.pallas import tpu as pltpu
from jax.sharding import PartitionSpec as P

MESH = pl.DeviceIdType.MESH

M2, M1, OWN, P1, P2, P3 = range(6)
EDGES = {
    0: (
        (OWN, 2, "y", M2), (OWN, 1, -3, P3), (OWN, 0, "c", M1),
        (P2, 2, 4, M2), (P2, 0, "c", P1), (M1, 2, "c", M2),
    ),
    1: (
        (OWN, 0, "y", M2), (OWN, 0, "c", P1),
        (P2, 0, 3, M1), (P2, 1, "c", P3), (P3, 1, "y", P1),
    ),
    2: (
        (OWN, 0, "y", P2), (OWN, 1, -3, P3), (OWN, 0, "c", M1),
        (M2, 2, -4, P2), (P2, 2, "c", P1),
    ),
    3: (
        (OWN, 0, "y", P2), (OWN, 0, "c", P1),
        (M2, 0, -4, P2), (M2, 0, "c", M1), (P2, 1, "c", P3), (P1, 1, "c", P2),
    ),
}
RELAYS = {
    0: ((P2, 0), (M1, 0)),
    1: ((P2, 0), (P3, 1)),
    2: ((M2, 2), (P2, 2)),
    3: ((M2, 0), (P1, 1), (P2, 0)),
}
COLUMN_PARTS = 2
BACK = {"y": "y", "c": "c", 3: -3, -3: 3, 4: -4, -4: 4}
MAX_EDGES = max(len(edges) for edges in EDGES.values())


def role_at(role, target):
    if target == "y":
        return role ^ 2
    if target in ("c", 3, -3):
        return role ^ 1
    return role


def arrivals():
    table = {role: {} for role in EDGES}
    for role, edges in EDGES.items():
        for number, (source, half, target, slot) in enumerate(edges):
            table[role_at(role, target)][slot, half] = (BACK[target], number)
    return table


ARRIVE = arrivals()


def place(target):
    me, count = lax.axis_index("row"), lax.axis_size("row")
    if target == "y":
        return me + 2 - 4 * (me // 2 % 2)
    if target == "c":
        return me + 1 - 2 * (me % 2)
    return (me + target + count) % count


def rows_of(slot, half, strip):
    if half == 0:
        return pl.ds(slot * strip, strip)
    return pl.ds(slot * strip + (half - 1) * (strip // 2), strip // 2)


def mark(key):
    return 2 * key[0] + (key[1] == 2)


def source_key(role, source, half):
    return (source, 0) if (source, 0) in ARRIVE[role] else (source, half)


def chunks_of(planes, columns):
    width = columns // COLUMN_PARTS
    return [(plane, pl.ds(part * width, width)) for plane in range(planes) for part in range(COLUMN_PARTS)]


def greet():
    me = lax.axis_index("row")
    barrier = pltpu.get_barrier_semaphore()
    for target in ("y", "c", 4, -4):
        pl.semaphore_signal(barrier, inc=1, device_id={"row": place(target)}, device_id_type=MESH)

    @pl.when(me % 2 == 0)
    def _():
        pl.semaphore_signal(barrier, inc=1, device_id={"row": place(-3)}, device_id_type=MESH)

    @pl.when(me % 2 == 1)
    def _():
        pl.semaphore_signal(barrier, inc=1, device_id={"row": place(3)}, device_id_type=MESH)

    pl.semaphore_wait(barrier, 5)


def table_rows(first, count, phase_ref, tables):
    left_real, left_imag, right_real, right_imag, prop_real, prop_imag = tables
    edge = phase_ref.shape[0]
    step = 16

    @pl.loop(0, count // step)
    def _(i):
        start = pl.multiple_of(first + i * step, step)
        rows, low, high = pl.ds(start, step), pl.ds(0, edge), pl.ds(edge, edge)
        more = pl.ds(pl.multiple_of(edge + start, step), step)
        line = lax.broadcasted_iota(jnp.int32, (step, edge), 0) + start
        index = line * lax.broadcasted_iota(jnp.int32, (step, edge), 1)
        wrapped = index & (edge - 1) if edge & (edge - 1) == 0 else lax.rem(index, edge)
        angles = wrapped.astype(jnp.float32) * (-2.0 * math.pi / edge)
        factor = 1.0 / math.sqrt(edge)
        cosine = (jnp.cos(angles) * factor).astype(jnp.bfloat16)
        plain = jnp.sin(angles) * factor
        sine, minus = plain.astype(jnp.bfloat16), (-plain).astype(jnp.bfloat16)
        left_real[rows, low] = cosine
        left_real[rows, high] = minus
        left_imag[rows, low] = sine
        left_imag[rows, high] = cosine
        right_real[rows, :] = cosine
        right_real[more, :] = minus
        right_imag[rows, :] = sine
        right_imag[more, :] = cosine
        prop_real[rows, :] = jnp.cos(phase_ref[rows, :])
        prop_imag[rows, :] = jnp.sin(phase_ref[rows, :])


def feeds(role, edge, key):
    source, half = edge[0], edge[1]
    if key is None:
        return source == OWN
    return source != OWN and source_key(role, source, half) == key


def gather_kernel(own_ref, phase_ref, out_ref, *refs):
    tables = refs[:6]
    send_sem, recv_sem, keep_sem = refs[6:]
    full = [out_ref.at[plane] for plane in range(own_ref.shape[0])]
    planes, strip, columns = own_ref.shape
    chunks = chunks_of(planes, columns)
    me = lax.axis_index("row")
    greet()

    def edge(role, number, chunk):
        source, half, target, slot = EDGES[role][number]
        plane, lanes = chunks[chunk]
        if source == OWN:
            origin = own_ref.at[plane, rows_of(0, half, strip), lanes]
        else:
            origin = full[plane].at[rows_of(source, half, strip), lanes]
        return pltpu.make_async_remote_copy(
            src_ref=origin,
            dst_ref=full[plane].at[rows_of(slot, half, strip), lanes],
            send_sem=send_sem.at[number, chunk],
            recv_sem=recv_sem.at[mark((slot, half)), chunk],
            device_id={"row": place(target)},
            device_id_type=MESH,
        )

    def arrived(role, key, chunk):
        back, _ = ARRIVE[role][key]
        plane, lanes = chunks[chunk]
        spot = full[plane].at[rows_of(*key, strip), lanes]
        pltpu.make_async_remote_copy(
            src_ref=spot,
            dst_ref=spot,
            send_sem=send_sem.at[0, chunk],
            recv_sem=recv_sem.at[mark(key), chunk],
            device_id={"row": place(back)},
            device_id_type=MESH,
        ).wait_recv()

    def launch(role, key, chunk):
        for number, entry in enumerate(EDGES[role]):
            if feeds(role, entry, key):
                edge(role, number, chunk).start()

    def begin(role):
        for chunk in range(len(chunks)):
            launch(role, None, chunk)

    def relay(role, step):
        for late, key in enumerate(RELAYS[role]):
            if 0 <= step - late < len(chunks):
                arrived(role, key, step - late)
                launch(role, key, step - late)

    def rest(role, plane):
        for chunk in range(plane * COLUMN_PARTS, (plane + 1) * COLUMN_PARTS):
            for key in ARRIVE[role]:
                if key not in RELAYS[role]:
                    arrived(role, key, chunk)

    def drain(role):
        for chunk in range(len(chunks)):
            for number in range(len(EDGES[role])):
                edge(role, number, chunk).wait_send()

    def by_role(work, *args):
        for role in EDGES:
            pl.when(me % 4 == role)(functools.partial(work, role, *args))

    by_role(begin)
    keeps = [
        pltpu.make_async_copy(
            own_ref.at[plane], full[plane].at[pl.ds(OWN * strip, strip)], keep_sem.at[plane]
        )
        for plane in range(planes)
    ]
    for keep in keeps:
        keep.start()
    share = phase_ref.shape[0] // len(chunks)
    late = max(len(relays) for relays in RELAYS.values()) - 1
    for step in range(len(chunks) + late):
        if step < len(chunks):
            table_rows(step * share, share, phase_ref, tables)
        by_role(relay, step)
    for plane in range(planes):
        by_role(rest, plane)
        keeps[plane].wait()
    by_role(drain)


def scatter_kernel(grad_ref, out_ref, total, held, send_sem, recv_sem, load_sem):
    planes, strip, columns = out_ref.shape
    chunks = chunks_of(planes, columns)
    loads = [
        pltpu.make_async_copy(grad_ref.at[plane], total.at[plane], load_sem.at[plane])
        for plane in range(planes)
    ]
    for load in loads:
        load.start()
    greet()

    def work(role):
        edges = EDGES[role]
        keys = ARRIVE[role]

        def returned(key, chunk):
            target, number = keys[key]
            plane, lanes = chunks[chunk]
            count = strip if key[1] == 0 else strip // 2
            return pltpu.make_async_remote_copy(
                src_ref=total.at[plane, rows_of(*key, strip), lanes],
                dst_ref=held.at[number, plane, pl.ds(0, count), lanes],
                send_sem=send_sem.at[mark(key), chunk],
                recv_sem=recv_sem.at[number, chunk],
                device_id={"row": place(target)},
                device_id_type=MESH,
            )

        def absorb(key, chunk):
            plane, lanes = chunks[chunk]
            for number, (source, half, target, _) in enumerate(edges):
                if not feeds(role, (source, half), key):
                    continue
                count = strip if half == 0 else strip // 2
                spot = held.at[number, plane, pl.ds(0, count), lanes]
                pltpu.make_async_remote_copy(
                    src_ref=spot,
                    dst_ref=spot,
                    send_sem=send_sem.at[0, chunk],
                    recv_sem=recv_sem.at[number, chunk],
                    device_id={"row": place(target)},
                    device_id_type=MESH,
                ).wait_recv()
                rows = rows_of(source, half, strip)
                total[plane, rows, lanes] = total[plane, rows, lanes] + held[number, plane, pl.ds(0, count), lanes]

        relays = RELAYS[role][::-1]
        order = [key for key in keys if key not in relays]
        order.sort(key=lambda key: (keys[key][0] == "c" and key[0] == M1, key[0]))
        for chunk in range(len(chunks)):
            if chunk % COLUMN_PARTS == 0:
                loads[chunks[chunk][0]].wait()
            for key in order:
                returned(key, chunk).start()
        for step in range(len(chunks) + len(relays) - 1):
            for late, key in enumerate(relays):
                if 0 <= step - late < len(chunks):
                    absorb(key, step - late)
                    returned(key, step - late).start()
        for chunk in range(len(chunks)):
            plane, lanes = chunks[chunk]
            absorb(None, chunk)
            out_ref[plane, :, lanes] = total[plane, pl.ds(OWN * strip, strip), lanes]
        for chunk in range(len(chunks)):
            for key in keys:
                returned(key, chunk).wait_send()

    me = lax.axis_index("row")
    for role in EDGES:
        pl.when(me % 4 == role)(functools.partial(work, role))


def extract_kernel(spot_ref, full_ref, out_ref):
    edge, columns = out_ref.shape[-1], full_ref.shape[-1]
    step = 64
    turn = (columns - spot_ref[1]) % columns
    past = spot_ref[0] % 8
    base = pl.multiple_of(spot_ref[0] - past, 8)

    @pl.loop(0, edge // step)
    def _(i):
        rows = full_ref[0, pl.ds(pl.multiple_of(base + i * step, 8), step + 8), :]
        rows = pltpu.roll(rows, turn, 1)[:, :edge]
        out_ref[0, pl.ds(i * step, step), :] = pltpu.roll(rows, (step + 8 - past) % (step + 8), 0)[:step]


def insert_kernel(spot_ref, grad_ref, out_ref, tall_ref):
    edge, (height, columns) = grad_ref.shape[-1], out_ref.shape[1:]
    step, lead = 64, height - edge
    past = spot_ref[0] % 8
    base = pl.multiple_of(spot_ref[0] - past, 8)
    out_ref[0, pl.ds(0, lead), :] = jnp.zeros((lead, columns), jnp.float32)
    out_ref[0, pl.ds(edge, lead), :] = jnp.zeros((lead, columns), jnp.float32)
    tall_ref[pl.ds(0, 8), :] = jnp.zeros((8, edge), jnp.float32)
    tall_ref[pl.ds(8, edge), :] = grad_ref[0]
    tall_ref[pl.ds(edge + 8, 8), :] = jnp.zeros((8, edge), jnp.float32)

    def move(i, count):
        rows = tall_ref[pl.ds(i * step, count + 8), :]
        rows = pltpu.roll(rows, count + past, 0)[:count]
        wide = jnp.concatenate([rows, jnp.zeros((count, columns - edge), jnp.float32)], axis=1)
        out_ref[0, pl.ds(pl.multiple_of(base + i * step, 8), count), :] = pltpu.roll(wide, spot_ref[1], 1)

    pl.loop(0, edge // step)(lambda i: move(i, step))
    move(edge // step, 8)


def gather(own, phase, height):
    planes, strip, columns = own.shape
    edge = phase.shape[0]
    left = jax.ShapeDtypeStruct((edge, 2 * edge), jnp.bfloat16)
    right = jax.ShapeDtypeStruct((2 * edge, edge), jnp.bfloat16)
    flat = jax.ShapeDtypeStruct((edge, edge), jnp.float32)
    vmem = pl.BlockSpec(memory_space=pltpu.VMEM)
    parts = planes * COLUMN_PARTS
    return pl.pallas_call(
        gather_kernel,
        name="gather",
        out_shape=[
            jax.ShapeDtypeStruct((planes, height, columns), jnp.float32),
            left, left, right, right, flat, flat,
        ],
        in_specs=[vmem, vmem],
        out_specs=[pl.BlockSpec(memory_space=pl.ANY)] + [vmem] * 6,
        scratch_shapes=[
            pltpu.SemaphoreType.DMA((MAX_EDGES, parts)),
            pltpu.SemaphoreType.DMA((12, parts)),
            pltpu.SemaphoreType.DMA((planes,)),
        ],
        compiler_params=pltpu.CompilerParams(collective_id=0, has_side_effects=True),
    )(own, phase)


def scatter(grads, strip):
    planes, height, columns = grads.shape
    return pl.pallas_call(
        scatter_kernel,
        name="scatter",
        out_shape=jax.ShapeDtypeStruct((planes, strip, columns), jnp.float32),
        in_specs=[pl.BlockSpec(memory_space=pl.ANY)],
        out_specs=pl.BlockSpec(memory_space=pltpu.VMEM),
        scratch_shapes=[
            pltpu.VMEM((planes, height, columns), jnp.float32),
            pltpu.VMEM((MAX_EDGES, planes, strip, columns), jnp.float32),
            pltpu.SemaphoreType.DMA((12, planes * COLUMN_PARTS)),
            pltpu.SemaphoreType.DMA((MAX_EDGES, planes * COLUMN_PARTS)),
            pltpu.SemaphoreType.DMA((planes,)),
        ],
        compiler_params=pltpu.CompilerParams(collective_id=1, has_side_effects=True),
    )(grads)


def local_move(kernel, name, spot, source, shape, scratch=()):
    planes = source.shape[0]
    return pl.pallas_call(
        kernel,
        name=name,
        out_shape=jax.ShapeDtypeStruct((planes, *shape), jnp.float32),
        grid_spec=pltpu.PrefetchScalarGridSpec(
            num_scalar_prefetch=1,
            grid=(planes,),
            in_specs=[pl.BlockSpec((1, *source.shape[1:]), lambda plane, spot: (plane, 0, 0))],
            out_specs=pl.BlockSpec((1, *shape), lambda plane, spot: (plane, 0, 0)),
            scratch_shapes=scratch,
        ),
    )(spot, source)


def transform(real_part, imag_part, mats):
    left_real, left_imag, right_real, right_imag = mats
    stacked = jnp.concatenate(
        [real_part.astype(jnp.bfloat16), imag_part.astype(jnp.bfloat16)], axis=0
    )
    half_real = jnp.dot(left_real, stacked, preferred_element_type=jnp.float32).astype(jnp.bfloat16)
    half_imag = jnp.dot(left_imag, stacked, preferred_element_type=jnp.float32).astype(jnp.bfloat16)
    joined = jnp.concatenate([half_real, half_imag], axis=1)
    return (
        jnp.dot(joined, right_real, preferred_element_type=jnp.float32),
        jnp.dot(joined, right_imag, preferred_element_type=jnp.float32),
    )


def cmul(a_real, a_imag, b_real, b_imag):
    return (a_real * b_real - a_imag * b_imag, a_real * b_imag + a_imag * b_real)


def cmul_conj(a_real, a_imag, b_real, b_imag):
    return (a_real * b_real + a_imag * b_imag, a_real * b_imag - a_imag * b_real)


def window_gradient(window, probe, amplitude, propagator, forward):
    prop_real, prop_imag = propagator
    probe_real, probe_imag = (probe[0], probe[1])
    first_real, first_imag = (window[0], window[1])
    second_real, second_imag = (window[2], window[3])
    exit_real, exit_imag = cmul(probe_real, probe_imag, first_real, first_imag)
    freq_real, freq_imag = transform(exit_real, exit_imag, forward)
    moved_real, moved_imag = cmul(freq_real, freq_imag, prop_real, prop_imag)
    inner_imag, inner_real = transform(moved_imag, moved_real, forward)
    wave_real, wave_imag = cmul(inner_real, inner_imag, second_real, second_imag)
    far_real, far_imag = transform(wave_real, wave_imag, forward)
    modulus = jnp.sqrt(far_real * far_real + far_imag * far_imag)
    ratio = amplitude / jnp.maximum(modulus, 0.1)
    resid_real = far_real * (1.0 - ratio)
    resid_imag = far_imag * (1.0 - ratio)
    back_imag, back_real = transform(resid_imag, resid_real, forward)
    grad2_real, grad2_imag = cmul_conj(inner_real, inner_imag, back_real, back_imag)
    mid_real, mid_imag = cmul_conj(second_real, second_imag, back_real, back_imag)
    spec_real, spec_imag = transform(mid_real, mid_imag, forward)
    unprop_real, unprop_imag = cmul_conj(prop_real, prop_imag, spec_real, spec_imag)
    entry_imag, entry_real = transform(unprop_imag, unprop_real, forward)
    grad1_real, grad1_imag = cmul_conj(probe_real, probe_imag, entry_real, entry_imag)
    return jnp.stack([grad1_real, grad1_imag, grad2_real, grad2_imag])


def body(object_field, row_offset, col_offset, amplitudes, probe, phase):
    strip, columns = object_field.shape[2:]
    edge = probe.shape[1]
    half = strip // 2
    height = 5 * strip + half
    own = object_field.reshape(4, strip, columns)
    spot = jnp.concatenate([row_offset + half, col_offset])
    around, *tables = gather(own, phase, height)
    forward, propagator = tables[:4], tables[4:]
    window = local_move(extract_kernel, "extract", spot, around, (edge, edge))
    grads = window_gradient(window, probe, amplitudes[0], propagator, forward)
    spread = local_move(
        insert_kernel, "insert", spot, grads, (height, columns),
        [pltpu.VMEM((edge + 16, edge), jnp.float32)],
    )
    total = scatter(spread, strip)
    return (own - 0.5 * total).reshape(object_field.shape)


def solution(mesh):
    placed = (
        P(None, None, ("scan", "row"), None),
        P(("scan", "row")),
        P(("scan", "row")),
        P(("scan", "row"), None, None),
        P("scan", None, None),
        P(),
    )
    return jax.shard_map(
        body,
        mesh=mesh,
        in_specs=placed,
        out_specs=P(None, None, ("scan", "row"), None),
        check_vma=False,
    )
```
